32 devices in a mesh: slab: 8 (over y, x, core), blk: 4 (over z).
Axes of the slice: x: 2, y: 2, z: 4, core: 2. Of those that a mesh axis runs over, the one named last changes fastest.
Arguments:
- start_block: float32 [128, 64, 8, 128], P('blk', 'slab'), as said below
- locked_modes: float32 [384, 64, 8, 128], P('blk', 'slab'), as said below
- material: int32 [64, 8, 128], P('slab'), may hold values 0 or 1
- support: int32 [8, 128], replicated, may hold values 0 or 1
Outputs:
- basis: float32 [128, 64, 8, 128], P('blk', 'slab')
The draws below stay inside these ranges and needn't reach their ends.
Inputs may be any that keep to these rules, and one draw needn't show every extreme that they name: `start_block`: A block of random vectors with large parts along the locked modes. `locked_modes`: each locked mode (one row) has about unit norm over all voxels.
All inputs are finite; a program needn't handle non-finite values. No bound on the sum of `material` on one device may be relied on, other than what follows from the above.
Results may differ from the reference program's by a relative error of at most 0.00014.
Values sent between devices are 32-bit elements; how exact they have to be, the bound alone decides.
No kernel may reach another device: no remote copies, remote signals or barrier semaphores. Data moves between devices by JAX's collectives and lax.ppermute only.
A program may use at most 64 MiB of HBM per device.

```python
import jax
import jax.numpy as jnp
from jax import lax

COLS = 128
LOCKED = 384
DEGREE = 8
NY = 8
NX = 128
NZ = 64


def locked_field(key):
    base = jax.random.fold_in(key, 101)
    shape = (LOCKED, NZ, NY, NX)
    values = jnp.clip(jax.random.normal(base, shape, jnp.float32), -6.0, 6.0)
    order = jax.random.permutation(jax.random.fold_in(key, 505), LOCKED).astype(jnp.int32)
    partner = jnp.zeros((LOCKED,), jnp.int32).at[order].set(jnp.roll(order, -1))
    coupled = values + 0.3 * values[partner]
    return coupled / jnp.sqrt(jnp.float32(1.09 * NZ * NY * NX))


def draw_locked_modes(key, part):
    return locked_field(key)


def draw_start_block(key, part):
    modes = locked_field(key)
    picks = jax.random.permutation(jax.random.fold_in(key, 202), LOCKED).reshape(COLS, 3)
    weights = jnp.clip(jax.random.normal(jax.random.fold_in(key, 303), (COLS, 3), jnp.float32), -3.0, 3.0)
    mixed = weights[:, 0, None, None, None] * modes[picks[:, 0]]
    mixed = mixed + weights[:, 1, None, None, None] * modes[picks[:, 1]]
    mixed = mixed + weights[:, 2, None, None, None] * modes[picks[:, 2]]
    noise = jnp.clip(jax.random.normal(jax.random.fold_in(key, 404), (COLS, NZ, NY, NX), jnp.float32), -6.0, 6.0)
    return jnp.sqrt(jnp.float32(NZ * NY * NX)) * mixed + 0.5 * noise


def touch_ends(entries, own_key, low, high):
    shape = entries.shape
    place = [jax.random.randint(jax.random.fold_in(own_key, axis), (), 0, shape[axis]) for axis in range(len(shape))]
    entries = entries.at[tuple(place)].set(low)
    longest = shape.index(max(shape))
    place[longest] = (place[longest] + 1) % shape[longest]
    return entries.at[tuple(place)].set(high)


def setup_inputs(seed: int = 0) -> dict:
    streams_of = jax.random.split(jax.random.key(seed), 5)
    return {
        "start_block": draw_start_block(jax.random.fold_in(streams_of[4], 71), 0),
        "locked_modes": draw_locked_modes(jax.random.fold_in(streams_of[4], 71), 0),
        "material": touch_ends((jax.random.randint(streams_of[2], (NZ, NY, NX), 0, 5) < 4).astype(jnp.int32), jax.random.fold_in(streams_of[2], 1), 0, 1),
        "support": touch_ends((jax.random.randint(streams_of[3], (NY, NX), 0, 2) < 1).astype(jnp.int32), jax.random.fold_in(streams_of[3], 1), 0, 1),
    }


THETA_LOAD = 0.1
VOID_ROOT = 0.31622776601683794
FILTER_CENTRE = 9.0
FILTER_HALF = 7.5

def blurred(padded):
    along_z = 0.5 * padded[:, :-2] + padded[:, 1:-1] + 0.5 * padded[:, 2:]
    along_y = 0.5 * along_z[:, :, :-2] + along_z[:, :, 1:-1] + 0.5 * along_z[:, :, 2:]
    along_x = 0.5 * along_y[..., :-2] + along_y[..., 1:-1] + 0.5 * along_y[..., 2:]
    return 2.0 * along_x

def operate(field, free_cells, root_stiff):
    kept_field = free_cells * field
    weighted = root_stiff * kept_field
    padded = jnp.pad(weighted, ((0, 0), (1, 1), (1, 1), (1, 1)))
    smooth = blurred(padded)
    neighbours = padded[:, 2:, 1:-1, 1:-1] + padded[:, :-2, 1:-1, 1:-1]
    elastic = root_stiff * (16.0 * weighted - smooth)
    geometric = THETA_LOAD * root_stiff * (2.0 * weighted - neighbours)
    return free_cells * (elastic - geometric + 0.5 * kept_field) + (1.0 - free_cells) * field

def reference(start_block, locked_modes, material, support):
    root_stiff = jnp.where(material == 1, 1.0, VOID_ROOT).astype(jnp.float32)
    layer = lax.broadcasted_iota(jnp.int32, material.shape, 0)
    clamped = jnp.where(layer == 0, support[None, :, :], 0)
    free_cells = (1 - clamped).astype(jnp.float32)
    previous = start_block
    current = (operate(start_block, free_cells, root_stiff) - FILTER_CENTRE * start_block) / FILTER_HALF
    for order_index in range(DEGREE - 1):
        following = 2.0 * (operate(current, free_cells, root_stiff) - FILTER_CENTRE * current) / FILTER_HALF - previous
        previous = current
        current = following
    cells = NZ * NY * NX
    flat = current.reshape(COLS, cells)
    modes_flat = locked_modes.reshape(LOCKED, cells)
    correlations = jnp.dot(modes_flat.astype(jnp.float32), flat.T.astype(jnp.float32), precision=lax.Precision.HIGHEST, preferred_element_type=jnp.float32)
    deflated = flat - jnp.dot(correlations.T.astype(jnp.float32), modes_flat.astype(jnp.float32), precision=lax.Precision.HIGHEST, preferred_element_type=jnp.float32)
    gram = jnp.dot(deflated.astype(jnp.float32), deflated.T.astype(jnp.float32), precision=lax.Precision.HIGHEST, preferred_element_type=jnp.float32)
    lower_factor = jnp.linalg.cholesky(gram)
    identity = jnp.eye(COLS, dtype=jnp.float32)
    inverse = jax.scipy.linalg.solve_triangular(lower_factor, identity, lower=True)
    basis = jnp.sqrt(jnp.float32(cells)) * jnp.dot(inverse.astype(jnp.float32), deflated.astype(jnp.float32), precision=lax.Precision.HIGHEST, preferred_element_type=jnp.float32)
    return basis.reshape(COLS, NZ, NY, NX)
```

```python
import jax
import jax.numpy as jnp
from jax import lax
from jax.experimental import pallas as pl
from jax.experimental.pallas import tpu as pltpu
from jax.sharding import PartitionSpec as P

DEGREE = 8
THETA_LOAD = 0.1
VOID_ROOT = 0.31622776601683794
FILTER_CENTRE = 9.0
FILTER_HALF = 7.5


HIGHEST = lax.Precision.HIGHEST
F32 = jnp.float32


def pairs(axis, bits):
    return [(i, i ^ bits) for i in range(lax.axis_size(axis))]


def swap(x, axis, bits):
    return lax.ppermute(x, axis, pairs(axis, bits))


def whole(shape):
    return pl.BlockSpec(shape, lambda *_: (0,) * len(shape))


def smem():
    return pl.BlockSpec(memory_space=pltpu.SMEM)


def filter_kernel(place, own, below, above, coef, first, *rest, steps, split):
    outs, field = rest[:-1], rest[-1]
    count, depth, ny, nx = own.shape
    halo = below.shape[1]
    total = depth + 2 * halo
    scale = 2.0 / FILTER_HALF
    row = lax.broadcasted_iota(jnp.int32, (ny, nx), 0)
    col = lax.broadcasted_iota(jnp.int32, (ny, nx), 1)
    up = jnp.where(row > 0, 0.5, 0.0).astype(F32)
    down = jnp.where(row < ny - 1, 0.5, 0.0).astype(F32)
    left = jnp.where(col > 0, 0.5, 0.0).astype(F32)
    right = jnp.where(col < nx - 1, 0.5, 0.0).astype(F32)
    bulk = F32(scale * (0.5 - FILTER_CENTRE))

    def one(v, carry):
        current = (
            [below[v, i] for i in range(halo)]
            + [own[v, i] for i in range(depth)]
            + [above[v, i] for i in range(halo)]
        )
        previous = None
        for step in range(steps):
            lo, hi = step + 1, total - 1 - step
            weighted = {i: coef[i] * current[i] for i in range(lo - 1, hi + 1)}
            following = [None] * total
            for i in range(lo, hi):
                near = weighted[i - 1] + weighted[i + 1]
                line = 0.5 * near + weighted[i]
                plane = line + up * pltpu.roll(line, 1, 0) + down * pltpu.roll(line, ny - 1, 0)
                cube = plane + left * pltpu.roll(plane, 1, 1) + right * pltpu.roll(plane, nx - 1, 1)
                rest_of = (8.0 - THETA_LOAD) * weighted[i] + (THETA_LOAD / 2) * near - cube
                plain = first[...] if i == halo else bulk
                new = coef[i] * rest_of + plain * current[i]
                following[i] = 0.5 * new if previous is None else new - previous[i]
            previous = current
            current = following
        for i in range(depth):
            field[v, i * ny : (i + 1) * ny, :] = current[halo + i]
        return carry

    lax.fori_loop(0, count, one, 0)
    if not split:
        outs[0][...] = field[...]
        return
    rows = outs[0].shape[1]
    for k, out in enumerate(outs):
        start = pl.multiple_of((place[0] ^ k) * rows, 8)
        out[...] = field[:, pl.ds(start, rows), :]


def filtered_parts(place, start_block, coef_own, first, parts):
    count, depth, ny, nx = start_block.shape
    halo = DEGREE
    assert depth >= halo
    slabs = lax.axis_size("slab")
    rise = [(i, i + 1) for i in range(slabs - 1)]
    fall = [(i + 1, i) for i in range(slabs - 1)]
    below = lax.ppermute(start_block[:, depth - halo :], "slab", rise)
    above = lax.ppermute(start_block[:, :halo], "slab", fall)
    coef_below = lax.ppermute(coef_own[depth - halo :], "slab", rise)
    coef_above = lax.ppermute(coef_own[:halo], "slab", fall)
    coef = jnp.concatenate([coef_below, coef_own, coef_above], axis=0)
    rows = depth * ny // parts
    split = rows % 8 == 0
    block = 8 if count % 8 == 0 else count
    if split:
        outs = [(count, rows, nx)] * parts
    else:
        outs = [(count, depth * ny, nx)]
    got = pl.pallas_call(
        lambda *refs: filter_kernel(*refs, steps=DEGREE, split=split),
        grid=(count // block,),
        in_specs=[
            smem(),
            pl.BlockSpec((block, depth, ny, nx), lambda g: (g, 0, 0, 0)),
            pl.BlockSpec((block, halo, ny, nx), lambda g: (g, 0, 0, 0)),
            pl.BlockSpec((block, halo, ny, nx), lambda g: (g, 0, 0, 0)),
            whole(coef.shape),
            whole(first.shape),
        ],
        out_specs=[pl.BlockSpec((block,) + s[1:], lambda g: (g, 0, 0)) for s in outs],
        out_shape=[jax.ShapeDtypeStruct(s, F32) for s in outs],
        scratch_shapes=[pltpu.VMEM((block, depth * ny, nx), F32)],
        name="chebyshev",
    )(place, start_block, below, above, coef, first)
    if split:
        return list(got)
    return sliced_parts(got[0], place[0], parts)


def sliced_parts(x, z, parts):
    rows = x.shape[1] // parts
    return [lax.dynamic_slice_in_dim(x, (z ^ k) * rows, rows, 1) for k in range(parts)]


def line_up(place, parts, out):
    total, cells = out.shape
    count = total // len(parts)
    nx = parts[0].shape[1]
    rows = cells // nx
    for k, part in enumerate(parts):
        start = pl.multiple_of((place[0] ^ k) * count, 8)
        for r in range(rows):
            out[pl.ds(start, count), r * nx : (r + 1) * nx] = part[pl.ds(r, count, stride=rows), :]


def modes_kernel(place, *refs):
    line_up(place, refs[:-1], refs[-1])


def halves(core, value, mine, other):
    size = mine.shape[0]

    @pl.when(core == 0)
    def _():
        mine[...] = value[:size]
        other[...] = value[size:]

    @pl.when(core == 1)
    def _():
        mine[...] = value[size:]
        other[...] = value[:size]


def joined(core, mine, other, out):
    size = mine.shape[0]

    @pl.when(core == 0)
    def _():
        out[:size] = mine[...]
        out[size:] = other[...]

    @pl.when(core == 1)
    def _():
        out[size:] = mine[...]
        out[:size] = other[...]


def correlate_kernel(place, modes, *refs):
    parts, (fields, mine, other) = refs[:-3], refs[-3:]
    line_up(place, parts, fields)
    value = lax.dot_general(
        modes[...], fields[...], (((1,), (1,)), ((), ())), precision=HIGHEST, preferred_element_type=F32
    )
    halves(place[1], value, mine, other)


def deflate_kernel(place, mine_in, other_in, modes, fields, deflated, mine, other, corr):
    joined(place[1], mine_in, other_in, corr)
    along = lax.dot_general(
        corr[...], modes[...], (((0,), (0,)), ((), ())), precision=HIGHEST, preferred_element_type=F32
    )
    deflated[...] = fields[...] - along
    value = lax.dot_general(
        deflated[...], deflated[...], (((1,), (1,)), ((), ())), precision=HIGHEST, preferred_element_type=F32
    )
    halves(place[1], value, mine, other)


def basis_kernel(place, inverse, deflated, *outs, scale):
    total, cells = deflated.shape
    count = total // len(outs)
    nx = outs[0].shape[1]
    rows = cells // nx
    value = scale * lax.dot_general(
        inverse[...], deflated[...], (((1,), (0,)), ((), ())), precision=HIGHEST, preferred_element_type=F32
    )
    for p in range(len(outs)):
        for k, out in enumerate(outs):

            @pl.when((place[0] ^ k) == p)
            def _(p=p, out=out):
                for r in range(rows):
                    out[pl.ds(r, count, stride=rows), :] = value[
                        p * count : (p + 1) * count, r * nx : (r + 1) * nx
                    ]


def call(kernel, name, place, args, outs, scratch=()):
    return pl.pallas_call(
        kernel,
        in_specs=[smem()] + [whole(a.shape) for a in args],
        out_specs=[whole(s) for s in outs],
        out_shape=[jax.ShapeDtypeStruct(s, F32) for s in outs],
        scratch_shapes=[pltpu.VMEM(s, F32) for s in scratch],
        name=name,
    )(place, *args)


def groups_of(size, first):
    bits = []
    while first < size:
        bits.append(first)
        first *= 2
    out = []
    while bits:
        take, bits = bits[:2], bits[2:]
        out.append(take if len(take) == 1 else [take[0], take[1], take[0] | take[1]])
    return out


def reduced(mine, other):
    x = mine + swap(other, "slab", 1)
    for axis, first in (("slab", 2), ("blk", 1)):
        for group in groups_of(lax.axis_size(axis), first):
            got = [swap(x, axis, bits) for bits in group]
            for g in got:
                x = x + g
    return x, swap(x, "slab", 1)


def lower_inverse(gram):
    lower_factor = jnp.linalg.cholesky(gram)
    identity = jnp.eye(gram.shape[0], dtype=jnp.float32)
    return jax.scipy.linalg.solve_triangular(lower_factor, identity, lower=True)


def per_device(start_block, locked_modes, material, support):
    depth, ny, nx = material.shape
    own_count = start_block.shape[0]
    own_modes = locked_modes.shape[0]
    parts = lax.axis_size("blk")
    slab, z = lax.axis_index("slab"), lax.axis_index("blk")
    place = jnp.stack([z, slab % 2]).astype(jnp.int32)
    rows = depth * ny // parts
    cells = rows * nx
    count = own_count * parts
    modes_count = own_modes * parts

    mode_parts = sliced_parts(locked_modes.reshape(own_modes, depth * ny, nx), z, parts)
    order = [k for k in range(parts) if k & (k - 1)] + [k for k in range(1, parts) if not k & (k - 1)]
    mode_parts = {k: mode_parts[k] if k == 0 else swap(mode_parts[k], "blk", k) for k in [0] + order}

    root_stiff = jnp.where(material == 1, 1.0, VOID_ROOT).astype(F32)
    free_first = jnp.where(slab == 0, 1 - support, 1).astype(F32)
    layer = lax.broadcasted_iota(jnp.int32, material.shape, 0)
    free_cells = jnp.where(layer == 0, free_first[None], 1.0)
    root_two = F32((4.0 / FILTER_HALF) ** 0.5)
    coef_own = root_two * free_cells * root_stiff
    first = F32(2.0 / FILTER_HALF) * (1.0 - 0.5 * free_first - FILTER_CENTRE)
    field_parts = filtered_parts(place, start_block, coef_own, first, parts)
    field_parts = {k: field_parts[k] if k == 0 else swap(field_parts[k], "blk", k) for k in [0] + order}

    flat = lambda x: x.reshape(-1, nx)
    (modes,) = call(
        modes_kernel, "modes", place, [flat(mode_parts[k]) for k in range(parts)], [(modes_count, cells)]
    )
    fields, mine, other = call(
        correlate_kernel,
        "correlate",
        place,
        [modes] + [flat(field_parts[k]) for k in range(parts)],
        [(count, cells), (modes_count // 2, count), (modes_count // 2, count)],
    )
    mine, other = reduced(mine, other)
    deflated, mine, other = call(
        deflate_kernel,
        "deflate",
        place,
        [mine, other, modes, fields],
        [(count, cells), (count // 2, count), (count // 2, count)],
        scratch=[(modes_count, count)],
    )
    mine, other = reduced(mine, other)
    low = place[1] == 0
    gram = jnp.concatenate([jnp.where(low, mine, other), jnp.where(low, other, mine)], axis=0)
    inverse = lower_inverse(gram)
    total_cells = depth * ny * nx * lax.axis_size("slab")
    scale = float(total_cells) ** 0.5
    outs = call(
        lambda *refs: basis_kernel(*refs, scale=scale),
        "basis",
        place,
        [inverse, deflated],
        [(own_count * rows, nx)] * parts,
    )
    outs = {k: outs[k] if k == 0 else swap(outs[k], "blk", k) for k in [0] + order}
    basis = jnp.zeros((own_count, depth * ny, nx), F32)
    for k in range(parts):
        piece = outs[k].reshape(own_count, rows, nx)
        basis = lax.dynamic_update_slice_in_dim(basis, piece, (z ^ k) * rows, 1)
    return basis.reshape(start_block.shape)


def solution(mesh):
    in_specs = (
        P("blk", "slab", None, None),
        P("blk", "slab", None, None),
        P("slab", None, None),
        P(),
    )
    out_specs = P("blk", "slab", None, None)
    return jax.shard_map(
        per_device, mesh=mesh, in_specs=in_specs, out_specs=out_specs, check_vma=False
    )
```

```python
import jax
import jax.numpy as jnp
from jax import lax
from jax.experimental import pallas as pl
from jax.experimental.pallas import tpu as pltpu
from jax.sharding import PartitionSpec as P

DEGREE = 8
THETA_LOAD = 0.1
VOID_ROOT = 0.31622776601683794
FILTER_CENTRE = 9.0
FILTER_HALF = 7.5


HIGHEST = lax.Precision.HIGHEST
F32 = jnp.float32
TILE = 8


def swap(x, axis, bits):
    return lax.ppermute(x, axis, [(i, i ^ bits) for i in range(lax.axis_size(axis))])


def whole(shape):
    return pl.BlockSpec(shape, lambda *_: (0,) * len(shape))


def smem():
    return pl.BlockSpec(memory_space=pltpu.SMEM)


def call(kernel, place, args, outs, scratch=()):
    return pl.pallas_call(
        kernel,
        in_specs=[smem()] + [whole(a.shape) for a in args],
        out_specs=[whole(s) for s in outs],
        out_shape=[jax.ShapeDtypeStruct(s, F32) for s in outs],
        scratch_shapes=[pltpu.VMEM(s, F32) for s in scratch],
    )(place, *args)


def dot(a, b, da, db):
    return lax.dot_general(
        a, b, (((da,), (db,)), ((), ())), precision=HIGHEST, preferred_element_type=F32
    )


def in_line(ref):
    return jnp.concatenate([ref[r] for r in range(ref.shape[0])], axis=1)


def near_kernel(place, modes, *outs, total):
    count = modes.shape[0] // total
    share = outs[0].shape[0]
    for k, out in enumerate(outs):
        start = (place[0] ^ (k + 1)) * share
        for i in range(share):
            out[i] = modes[pl.ds(start + i, count, stride=total), :]


def far_kernel(place, modes, near, far, *outs, total):
    count = modes.shape[0] // total
    share = near.shape[0]
    start = place[0] * share
    for i in range(share):
        near[i] = modes[pl.ds(start + i, count, stride=total), :]
    first = total - far.shape[0]
    for i in range(far.shape[0]):
        far[i] = modes[pl.ds(first + i, count, stride=total), :]
    share = outs[0].shape[0]
    for k, out in enumerate(outs):
        start = first + (place[0] ^ k) * share
        for i in range(share):
            out[i] = modes[pl.ds(start + i, count, stride=total), :]


def split_modes(kernel, place, modes, outs, block):
    total = modes.shape[0] // outs[0][1]
    nx = modes.shape[1]
    return pl.pallas_call(
        lambda *refs: kernel(*refs, total=total),
        grid=(outs[0][1] // block,),
        in_specs=[smem(), pl.BlockSpec((block * total, nx), lambda g: (g, 0))],
        out_specs=[pl.BlockSpec((s[0], block, nx), lambda g: (0, g, 0)) for s in outs],
        out_shape=[jax.ShapeDtypeStruct(s, F32) for s in outs],
    )(place, modes)


def filter_kernel(place, own, below, above, coef_own, coef_below, coef_above, clamped, *rest, steps, ny):
    outs, (one, two, square, mixed, back) = rest[:-5], rest[-5:]
    nx = own.shape[1]
    depth = coef_own.shape[0]
    halo = coef_below.shape[0]
    total = depth + 2 * halo
    scale = 2.0 / FILTER_HALF
    col = lax.broadcasted_iota(jnp.int32, (TILE, nx), 1)
    left = jnp.where(col > 0, 0.5, 0.0).astype(F32)
    right = jnp.where(col < nx - 1, 0.5, 0.0).astype(F32)
    bulk = F32(scale * (0.5 - FILTER_CENTRE))
    near = F32(THETA_LOAD)
    centre = F32(16.0 - 4.0 * THETA_LOAD)

    @pl.when(pl.program_id(0) == 0)
    def _():
        for i in range(total):
            if i < halo:
                coef = coef_below[i]
            elif i < halo + depth:
                coef = coef_own[i - halo]
            else:
                coef = coef_above[i - halo - depth]
            for y in range(ny):
                row = jnp.broadcast_to(coef[y : y + 1, :], (TILE, nx))
                weight = F32(scale) * row * row
                square[i, y] = weight
                mixed[i, y] = centre * weight + bulk
                if halo <= i < halo + depth:
                    back[i - halo, y] = jnp.where(row > 0, 1.0 / jnp.where(row > 0, row, 1.0), 0.0)

    for i in range(total):
        if i < halo:
            source, base, layers, coef = below, i, halo, coef_below[i]
        elif i < halo + depth:
            source, base, layers, coef = own, i - halo, depth, coef_own[i - halo]
        else:
            source, base, layers, coef = above, i - halo - depth, halo, coef_above[i - halo - depth]
        for y in range(ny):
            value = source[pl.ds(base * ny + y, TILE, stride=layers * ny), :]
            one[i, y] = jnp.broadcast_to(coef[y : y + 1, :], (TILE, nx)) * value

    current, previous = one, two
    for step in range(steps):
        lo, hi = step + 1, total - 1 - step

        def layer(i, carry, step=step, current=current, previous=previous):
            here, pair = carry
            after = [current[i + 1, y] for y in range(ny)]
            pair_after = [here[y] + after[y] for y in range(ny)]
            line = [pair[y] + pair_after[y] for y in range(ny)]
            across = [line[y] + line[y + 1] for y in range(ny - 1)]
            for y in range(ny):
                if y == 0:
                    plane = across[0] + line[0]
                elif y == ny - 1:
                    plane = across[y - 1] + line[y]
                else:
                    plane = across[y - 1] + across[y]
                cube = plane + left * pltpu.roll(plane, 1, 1) + right * pltpu.roll(plane, nx - 1, 1)
                new = mixed[i, y] * here[y] + square[i, y] * (near * line[y] - 0.5 * cube)
                if step == 0:
                    previous[i, y] = 0.5 * new
                else:
                    previous[i, y] = new - previous[i, y]
            return after, pair_after

        before = [current[lo - 1, y] for y in range(ny)]
        here = [current[lo, y] for y in range(ny)]
        carry = (here, [before[y] + here[y] for y in range(ny)])
        for i in range(lo, hi):
            carry = layer(i, carry)
        current, previous = previous, current

    before, now = 1.0, (1.0 - FILTER_CENTRE) / FILTER_HALF
    for _ in range(steps - 1):
        before, now = now, 2.0 * now * (1.0 - FILTER_CENTRE) / FILTER_HALF - before
    for i in range(depth):
        for y in range(ny):
            value = back[i, y] * current[halo + i, y]
            if i == 0:
                fixed = jnp.broadcast_to(clamped[y : y + 1, :], (TILE, nx))
                value = value + F32(now) * fixed * own[pl.ds(y, TILE, stride=depth * ny), :]
            previous[i, y] = value
    rows = previous.reshape(total * ny, TILE, nx)
    far = outs[-1]
    far[...] = rows[pl.ds(depth * ny - far.shape[0], far.shape[0])]
    for k, out in enumerate(outs[:-1]):
        out[...] = rows[pl.ds((place[0] ^ k) * out.shape[0], out.shape[0])]


def filtered_rows(place, start_block, coef_own, clamped, near_rows, far_rows, parts):
    count, depth, ny, nx = start_block.shape
    halo = DEGREE
    assert depth >= halo and count % TILE == 0
    slabs = lax.axis_size("slab")
    rise = [(i, i + 1) for i in range(slabs - 1)]
    fall = [(i + 1, i) for i in range(slabs - 1)]
    below = lax.ppermute(start_block[:, depth - halo :], "slab", rise)
    above = lax.ppermute(start_block[:, :halo], "slab", fall)
    coef_below = lax.ppermute(coef_own[depth - halo :], "slab", rise)
    coef_above = lax.ppermute(coef_own[:halo], "slab", fall)
    outs = [(near_rows // parts, count, nx)] * parts + [(far_rows, count, nx)]
    total = depth + 2 * halo
    got = pl.pallas_call(
        lambda *refs: filter_kernel(*refs, steps=DEGREE, ny=ny),
        grid=(count // TILE,),
        in_specs=[smem()]
        + [pl.BlockSpec((TILE * n * ny, nx), lambda g: (g, 0)) for n in (depth, halo, halo)]
        + [whole(c.shape) for c in (coef_own, coef_below, coef_above, clamped)],
        out_specs=[pl.BlockSpec((s[0], TILE, nx), lambda g: (0, g, 0)) for s in outs],
        out_shape=[jax.ShapeDtypeStruct(s, F32) for s in outs],
        scratch_shapes=[pltpu.VMEM((total, ny, TILE, nx), F32)] * 4 + [pltpu.VMEM((depth, ny, TILE, nx), F32)],
        name="chebyshev",
    )(
        place,
        start_block.reshape(-1, nx),
        below.reshape(-1, nx),
        above.reshape(-1, nx),
        coef_own,
        coef_below,
        coef_above,
        clamped,
    )
    return list(got[:-1]), got[-1]


def gather_fields(place, parts, fields):
    count = parts[0].shape[1]
    for k, part in enumerate(parts):
        start = pl.multiple_of((place[0] ^ k) * count, TILE)
        fields[:, pl.ds(start, count), :] = part[...]


def near_correlate_kernel(place, *refs, parts):
    modes, pieces, fields, outs = refs[:parts], refs[parts : 2 * parts], refs[2 * parts], refs[2 * parts + 1 :]
    gather_fields(place, pieces, fields)
    own = in_line(fields)
    stack = jnp.concatenate([in_line(m) for m in modes], axis=0)
    value = dot(stack, own, 1, 1)
    size = outs[0].shape[0]
    for k, out in enumerate(outs):
        out[...] = value[k * size : (k + 1) * size]


def far_correlate_kernel(place, modes, *refs, parts):
    pieces, sums, fields, out = refs[:parts], refs[parts : 2 * parts], refs[2 * parts], refs[2 * parts + 1]
    gather_fields(place, pieces, fields)
    value = dot(in_line(modes), in_line(fields), 1, 1)
    for s in sums:
        value = value + s[...]
    out[...] = value


def halves(core, value, mine, other):
    size = mine.shape[0]

    @pl.when(core == 0)
    def _():
        mine[...] = value[:size]
        other[...] = value[size:]

    @pl.when(core == 1)
    def _():
        mine[...] = value[size:]
        other[...] = value[:size]


def deflate_kernel(place, *refs, parts):
    corr, near, far = refs[:parts], refs[parts : 2 * parts], refs[2 * parts : 3 * parts]
    near_fields, far_fields, deflated, mine, other = refs[3 * parts :]
    share = far[0].shape[0]
    fields = [near_fields[r] for r in range(near_fields.shape[0])]
    fields += [far_fields[place[0] * share + r] for r in range(share)]
    modes = jnp.concatenate(
        [jnp.concatenate([in_line(a), in_line(b)], axis=1) for a, b in zip(near, far)], axis=0
    )
    stack = jnp.concatenate([c[...] for c in corr], axis=0)
    value = jnp.concatenate(fields, axis=1) - dot(stack, modes, 0, 0)
    deflated[...] = value
    halves(place[1], dot(value, value, 1, 1), mine, other)


def lower_inverse(aug, out, count):
    tile, block = TILE, min(64, count)
    row = lax.broadcasted_iota(jnp.int32, (tile, count), 0)
    for top in range(0, count, block):
        q = block // tile
        left = [aug[top + i * tile : top + (i + 1) * tile, :count] for i in range(q)]
        right = [aug[top + i * tile : top + (i + 1) * tile, count:] for i in range(q)]
        for i in range(q):
            first = top + i * tile
            cols = {
                j: [jnp.broadcast_to(left[j][:, first + s : first + s + 1], (tile, count)) for s in range(tile)]
                for j in range(i, q)
            }
            roots = jnp.zeros((tile, count), F32)
            for t in range(tile):
                pick = lambda x: jnp.broadcast_to(x[t : t + 1, :], (tile, count))
                pivot = pick(cols[i][t])
                roots = jnp.where(row == t, lax.rsqrt(pivot), roots)
                over = 1.0 / pivot
                heads = {s: pick(cols[i][s]) for s in range(t + 1, tile)}
                head_left, head_right = pick(left[i]), pick(right[i])
                for j in range(i, q):
                    factor = cols[j][t] * over
                    if j == i:
                        factor = jnp.where(row > t, factor, 0.0)
                    for s in range(t + 1, tile):
                        cols[j][s] = cols[j][s] - factor * heads[s]
                    left[j] = left[j] - factor * head_left
                    right[j] = right[j] - factor * head_right
            left[i] = left[i] * roots
            right[i] = right[i] * roots
            out[first : first + tile, :] = right[i]
        low = top + block
        if low < count:
            upper = jnp.concatenate(left, axis=0)
            lane = lax.broadcasted_iota(jnp.int32, upper.shape, 1)
            both = jnp.concatenate([upper, jnp.concatenate(right, axis=0)], axis=1)
            change = dot(jnp.where(lane >= low, upper, 0.0), both, 0, 0)
            aug[low:, :] = aug[low:, :] - change[low:, :]


def basis_kernel(place, mine, other, deflated, *rest, scale):
    outs, aug, inverse = rest[:-2], rest[-2], rest[-1]
    count = deflated.shape[0]
    half = mine.shape[0]

    @pl.when(place[1] == 0)
    def _():
        aug[:half, :count] = mine[...]
        aug[half:, :count] = other[...]

    @pl.when(place[1] == 1)
    def _():
        aug[half:, :count] = mine[...]
        aug[:half, :count] = other[...]

    r = lax.broadcasted_iota(jnp.int32, (count, count), 0)
    c = lax.broadcasted_iota(jnp.int32, (count, count), 1)
    aug[:, count:] = jnp.where(r == c, 1.0, 0.0).astype(F32)
    lower_inverse(aug, inverse, count)
    rows, size, nx = outs[0].shape
    order = [
        inverse[pl.ds(pl.multiple_of((place[0] ^ k) * size, TILE), size), :] for k in range(len(outs))
    ]
    value = dot(scale * jnp.concatenate(order, axis=0), deflated[...], 1, 0)
    for k, out in enumerate(outs):
        for i in range(rows):
            out[i] = value[k * size : (k + 1) * size, i * nx : (i + 1) * nx]


def place_kernel(place, *refs, near_share, far_share, near_rows):
    parts, out = refs[:-1], refs[-1]
    count, _ = parts[0].shape[1:]
    total = out.shape[0] // count
    for k, part in enumerate(parts):
        for i in range(near_share + far_share):
            if i < near_share:
                row = (place[0] ^ k) * near_share + i
            else:
                row = near_rows + (place[0] ^ k) * far_share + i - near_share
            out[pl.ds(row, count, stride=total), :] = part[i]


def groups_of(size, first):
    bits = []
    while first < size:
        bits.append(first)
        first *= 2
    out = []
    while bits:
        take, bits = bits[:2], bits[2:]
        out.append(take if len(take) == 1 else [take[0], take[1], take[0] | take[1]])
    return out


def summed(x, axis, first):
    for group in groups_of(lax.axis_size(axis), first):
        got = [swap(x, axis, bits) for bits in group]
        for g in got:
            x = x + g
    return x


def order_of(parts):
    far = [k for k in range(parts) if 2 * k >= parts]
    return far + [k for k in range(1, parts) if 2 * k < parts]


def per_device(start_block, locked_modes, material, support):
    depth, ny, nx = material.shape
    own_count, own_modes = start_block.shape[0], locked_modes.shape[0]
    parts = lax.axis_size("blk")
    slab, z = lax.axis_index("slab"), lax.axis_index("blk")
    place = jnp.stack([z, slab % 2]).astype(jnp.int32)
    rows = depth * ny
    far_share = max(1, rows // (4 * parts))
    far_rows = far_share * parts
    near_rows = rows - far_rows
    near_share = near_rows // parts
    count = own_count * parts
    ks = range(parts)
    order = order_of(parts)

    def exchanged(pieces):
        got = {k: swap(pieces[k], "blk", k) for k in order}
        return [got[k] if k else pieces[0] for k in ks]

    def gathered(piece):
        have, bit = {0: piece}, parts // 2
        while bit:
            got = {k ^ bit: swap(x, "blk", bit) for k, x in have.items()}
            have |= got
            bit //= 2
        return [have[k] for k in ks]

    modes = locked_modes.reshape(-1, nx)
    block = own_modes // 2 if own_modes % (2 * TILE) == 0 else own_modes
    near_modes = split_modes(
        near_kernel, place, modes, [(near_share, own_modes, nx)] * (parts - 1), block
    )
    start_block, *near_modes = lax.optimization_barrier([start_block] + list(near_modes))
    near_modes = exchanged([None] + near_modes)
    near_modes[0], far_own, *far_modes = split_modes(
        far_kernel,
        place,
        modes,
        [(near_share, own_modes, nx), (far_rows, own_modes, nx)] + [(far_share, own_modes, nx)] * parts,
        block,
    )

    root_stiff = jnp.where(material == 1, 1.0, VOID_ROOT).astype(F32)
    clamped = jnp.where(slab == 0, support, 0).astype(F32)
    layer = lax.broadcasted_iota(jnp.int32, material.shape, 0)
    coef_own = jnp.where(layer == 0, 1.0 - clamped[None], 1.0) * root_stiff
    near_fields, far_field = filtered_rows(
        place, start_block, coef_own, clamped, near_rows, far_rows, parts
    )
    near_fields = exchanged(near_fields)
    far_field, *near_fields = lax.optimization_barrier([far_field] + near_fields)
    far_fields = gathered(far_field)

    near_all, *sums = call(
        lambda *refs: near_correlate_kernel(*refs, parts=parts),
        place,
        near_modes + near_fields,
        [(near_share, count, nx)] + [(own_modes, count)] * parts,
    )
    sums = exchanged(sums)
    middle = parts // 2
    *far_modes, far_fields[middle] = lax.optimization_barrier(far_modes + [far_fields[middle]])
    far_modes = exchanged(far_modes)
    far_all, corr = call(
        lambda *refs: far_correlate_kernel(*refs, parts=parts),
        place,
        [far_own] + far_fields + sums,
        [(far_rows, count, nx), (own_modes, count)],
    )
    corr = corr + swap(corr, "slab", 1)
    corr = summed(corr, "slab", 2)
    corr = exchanged([corr] * parts)
    deflated, mine, other = call(
        lambda *refs: deflate_kernel(*refs, parts=parts),
        place,
        corr + near_modes + far_modes + [near_all, far_all],
        [(count, (near_share + far_share) * nx), (count // 2, count), (count // 2, count)],
    )
    gram = summed(summed(mine + swap(other, "slab", 1), "slab", 2), "blk", 1)
    total_cells = rows * nx * lax.axis_size("slab")
    scale = float(total_cells) ** 0.5
    outs = call(
        lambda *refs: basis_kernel(*refs, scale=scale),
        place,
        [gram, swap(gram, "slab", 1), deflated],
        [(near_share + far_share, own_count, nx)] * parts,
        scratch=[(count, 2 * count), (count, count)],
    )
    outs = exchanged(list(outs))
    (basis,) = call(
        lambda *refs: place_kernel(*refs, near_share=near_share, far_share=far_share, near_rows=near_rows),
        place,
        outs,
        [(own_count * rows, nx)],
    )
    return basis.reshape(start_block.shape)


def solution(mesh):
    in_specs = (
        P("blk", "slab", None, None),
        P("blk", "slab", None, None),
        P("slab", None, None),
        P(),
    )
    out_specs = P("blk", "slab", None, None)

    return jax.shard_map(
        per_device, mesh=mesh, in_specs=in_specs, out_specs=out_specs, check_vma=False
    )
```

```python
import jax
import jax.numpy as jnp
from jax import lax
from jax.experimental import pallas as pl
from jax.experimental.pallas import tpu as pltpu
from jax.sharding import PartitionSpec as P

DEGREE = 8
THETA_LOAD = 0.1
VOID_ROOT = 0.31622776601683794
FILTER_CENTRE = 9.0
FILTER_HALF = 7.5


HIGHEST = lax.Precision.HIGHEST
F32 = jnp.float32
TILE = 8


def swap(x, axis, bits):
    return lax.ppermute(x, axis, [(i, i ^ bits) for i in range(lax.axis_size(axis))])


def whole(shape):
    return pl.BlockSpec(shape, lambda *_: (0,) * len(shape))


def smem():
    return pl.BlockSpec(memory_space=pltpu.SMEM)


def call(kernel, place, args, outs, scratch=()):
    return pl.pallas_call(
        kernel,
        in_specs=[smem()] + [whole(a.shape) for a in args],
        out_specs=[whole(s) for s in outs],
        out_shape=[jax.ShapeDtypeStruct(s, F32) for s in outs],
        scratch_shapes=[pltpu.VMEM(s, F32) for s in scratch],
    )(place, *args)


def dot(a, b, da, db):
    return lax.dot_general(
        a, b, (((da,), (db,)), ((), ())), precision=HIGHEST, preferred_element_type=F32
    )


def halved(x):
    high = x.astype(jnp.bfloat16)
    return high, (x - high.astype(F32)).astype(jnp.bfloat16)


def dot3(a, b, da, db):
    (ah, al), (bh, bl) = halved(a), halved(b)
    one = lambda x, y: lax.dot_general(
        x, y, (((da,), (db,)), ((), ())), preferred_element_type=F32
    )
    return one(ah, bh) + (one(ah, bl) + one(al, bh))


def in_line(ref):
    return jnp.concatenate([ref[r] for r in range(ref.shape[0])], axis=1)


def near_kernel(place, modes, *outs, total, ks):
    count = modes.shape[0] // total
    share = outs[0].shape[0]
    for k, out in zip(ks, outs):
        start = (place[0] ^ k) * share
        for i in range(share):
            out[i] = modes[pl.ds(start + i, count, stride=total), :]


def far_kernel(place, modes, near, far, *outs, total):
    count = modes.shape[0] // total
    share = near.shape[0]
    start = place[0] * share
    for i in range(share):
        near[i] = modes[pl.ds(start + i, count, stride=total), :]
    first = total - far.shape[0]
    for i in range(far.shape[0]):
        far[i] = modes[pl.ds(first + i, count, stride=total), :]
    share = outs[0].shape[0]
    for k, out in enumerate(outs):
        start = first + (place[0] ^ k) * share
        for i in range(share):
            out[i] = modes[pl.ds(start + i, count, stride=total), :]


def split_modes(kernel, place, modes, outs, block):
    total = modes.shape[0] // outs[0][1]
    nx = modes.shape[1]
    return pl.pallas_call(
        lambda *refs: kernel(*refs, total=total),
        grid=(outs[0][1] // block,),
        in_specs=[smem(), pl.BlockSpec((block * total, nx), lambda g: (g, 0))],
        out_specs=[pl.BlockSpec((s[0], block, nx), lambda g: (0, g, 0)) for s in outs],
        out_shape=[jax.ShapeDtypeStruct(s, F32) for s in outs],
    )(place, modes)


def filter_kernel(place, own, below, above, coef_own, coef_below, coef_above, clamped, *rest, steps, ny):
    outs, (one, two, square, mixed, back) = rest[:-5], rest[-5:]
    nx = own.shape[1]
    depth = coef_own.shape[0]
    halo = coef_below.shape[0]
    total = depth + 2 * halo
    scale = 2.0 / FILTER_HALF
    col = lax.broadcasted_iota(jnp.int32, (TILE, nx), 1)
    left = jnp.where(col > 0, 0.5, 0.0).astype(F32)
    right = jnp.where(col < nx - 1, 0.5, 0.0).astype(F32)
    bulk = F32(scale * (0.5 - FILTER_CENTRE))
    near = F32(THETA_LOAD)
    centre = F32(16.0 - 4.0 * THETA_LOAD)

    @pl.when(pl.program_id(0) == 0)
    def _():
        for i in range(total):
            if i < halo:
                coef = coef_below[i]
            elif i < halo + depth:
                coef = coef_own[i - halo]
            else:
                coef = coef_above[i - halo - depth]
            for y in range(ny):
                row = jnp.broadcast_to(coef[y : y + 1, :], (TILE, nx))
                weight = F32(scale) * row * row
                square[i, y] = weight
                mixed[i, y] = centre * weight + bulk
                if halo <= i < halo + depth:
                    back[i - halo, y] = jnp.where(row > 0, 1.0 / jnp.where(row > 0, row, 1.0), 0.0)

    for i in range(total):
        if i < halo:
            source, base, layers, coef = below, i, halo, coef_below[i]
        elif i < halo + depth:
            source, base, layers, coef = own, i - halo, depth, coef_own[i - halo]
        else:
            source, base, layers, coef = above, i - halo - depth, halo, coef_above[i - halo - depth]
        for y in range(ny):
            value = source[pl.ds(base * ny + y, TILE, stride=layers * ny), :]
            one[i, y] = jnp.broadcast_to(coef[y : y + 1, :], (TILE, nx)) * value

    current, previous = one, two
    for step in range(steps):
        lo, hi = step + 1, total - 1 - step

        def layer(i, carry, step=step, current=current, previous=previous):
            here, pair = carry
            after = [current[i + 1, y] for y in range(ny)]
            pair_after = [here[y] + after[y] for y in range(ny)]
            line = [pair[y] + pair_after[y] for y in range(ny)]
            across = [line[y] + line[y + 1] for y in range(ny - 1)]
            for y in range(ny):
                if y == 0:
                    plane = across[0] + line[0]
                elif y == ny - 1:
                    plane = across[y - 1] + line[y]
                else:
                    plane = across[y - 1] + across[y]
                cube = plane + left * pltpu.roll(plane, 1, 1) + right * pltpu.roll(plane, nx - 1, 1)
                new = mixed[i, y] * here[y] + square[i, y] * (near * line[y] - 0.5 * cube)
                if step == 0:
                    previous[i, y] = 0.5 * new
                else:
                    previous[i, y] = new - previous[i, y]
            return after, pair_after

        before = [current[lo - 1, y] for y in range(ny)]
        here = [current[lo, y] for y in range(ny)]
        carry = (here, [before[y] + here[y] for y in range(ny)])
        for i in range(lo, hi):
            carry = layer(i, carry)
        current, previous = previous, current

    before, now = 1.0, (1.0 - FILTER_CENTRE) / FILTER_HALF
    for _ in range(steps - 1):
        before, now = now, 2.0 * now * (1.0 - FILTER_CENTRE) / FILTER_HALF - before
    for i in range(depth):
        for y in range(ny):
            value = back[i, y] * current[halo + i, y]
            if i == 0:
                fixed = jnp.broadcast_to(clamped[y : y + 1, :], (TILE, nx))
                value = value + F32(now) * fixed * own[pl.ds(y, TILE, stride=depth * ny), :]
            previous[i, y] = value
    rows = previous.reshape(total * ny, TILE, nx)
    far = outs[-1]
    far[...] = rows[pl.ds(depth * ny - far.shape[0], far.shape[0])]
    for k, out in enumerate(outs[:-1]):
        out[...] = rows[pl.ds((place[0] ^ k) * out.shape[0], out.shape[0])]


def filtered_rows(place, start_block, coef_own, clamped, near_rows, far_rows, parts):
    count, depth, ny, nx = start_block.shape
    halo = DEGREE
    assert depth >= halo and count % TILE == 0
    slabs = lax.axis_size("slab")
    rise = [(i, i + 1) for i in range(slabs - 1)]
    fall = [(i + 1, i) for i in range(slabs - 1)]
    below = lax.ppermute(start_block[:, depth - halo :], "slab", rise)
    above = lax.ppermute(start_block[:, :halo], "slab", fall)
    coef_below = lax.ppermute(coef_own[depth - halo :], "slab", rise)
    coef_above = lax.ppermute(coef_own[:halo], "slab", fall)
    outs = [(near_rows // parts, count, nx)] * parts + [(far_rows, count, nx)]
    total = depth + 2 * halo
    got = pl.pallas_call(
        lambda *refs: filter_kernel(*refs, steps=DEGREE, ny=ny),
        grid=(count // TILE,),
        in_specs=[smem()]
        + [pl.BlockSpec((TILE * n * ny, nx), lambda g: (g, 0)) for n in (depth, halo, halo)]
        + [whole(c.shape) for c in (coef_own, coef_below, coef_above, clamped)],
        out_specs=[pl.BlockSpec((s[0], TILE, nx), lambda g: (0, g, 0)) for s in outs],
        out_shape=[jax.ShapeDtypeStruct(s, F32) for s in outs],
        scratch_shapes=[pltpu.VMEM((total, ny, TILE, nx), F32)] * 4 + [pltpu.VMEM((depth, ny, TILE, nx), F32)],
        name="chebyshev",
    )(
        place,
        start_block.reshape(-1, nx),
        below.reshape(-1, nx),
        above.reshape(-1, nx),
        coef_own,
        coef_below,
        coef_above,
        clamped,
    )
    return list(got[:-1]), got[-1]


def gather_fields(place, parts, fields):
    count = parts[0].shape[1]
    for k, part in enumerate(parts):
        start = pl.multiple_of((place[0] ^ k) * count, TILE)
        fields[:, pl.ds(start, count), :] = part[...]


def near_correlate_kernel(place, *refs, parts):
    modes, pieces, fields, outs = refs[:parts], refs[parts : 2 * parts], refs[2 * parts], refs[2 * parts + 1 :]
    gather_fields(place, pieces, fields)
    own = in_line(fields)
    stack = jnp.concatenate([in_line(m) for m in modes], axis=0)
    value = dot3(stack, own, 1, 1)
    size = outs[0].shape[0]
    for k, out in enumerate(outs):
        out[...] = value[k * size : (k + 1) * size]


def far_correlate_kernel(place, modes, *refs, parts):
    pieces, sums, fields, out = refs[:parts], refs[parts : 2 * parts], refs[2 * parts], refs[2 * parts + 1]
    gather_fields(place, pieces, fields)
    value = dot3(in_line(modes), in_line(fields), 1, 1)
    for s in sums:
        value = value + s[...]
    out[...] = value


def halves(core, value, mine, other):
    size = mine.shape[0]

    @pl.when(core == 0)
    def _():
        mine[...] = value[:size]
        other[...] = value[size:]

    @pl.when(core == 1)
    def _():
        mine[...] = value[size:]
        other[...] = value[:size]


def deflate_kernel(place, *refs, parts):
    corr, near, far = refs[:parts], refs[parts : 2 * parts], refs[2 * parts : 3 * parts]
    near_fields, far_fields, deflated, mine, other = refs[3 * parts :]
    share = far[0].shape[0]
    fields = [near_fields[r] for r in range(near_fields.shape[0])]
    fields += [far_fields[place[0] * share + r] for r in range(share)]
    modes = jnp.concatenate(
        [jnp.concatenate([in_line(a), in_line(b)], axis=1) for a, b in zip(near, far)], axis=0
    )
    stack = jnp.concatenate([c[...] for c in corr], axis=0)
    value = jnp.concatenate(fields, axis=1) - dot3(stack, modes, 0, 0)
    deflated[...] = value
    halves(place[1], dot3(value, value, 1, 1), mine, other)


def lower_inverse(aug, out, count):
    tile, block = TILE, min(64, count)
    row = lax.broadcasted_iota(jnp.int32, (tile, count), 0)
    for top in range(0, count, block):
        q = block // tile
        left = [aug[top + i * tile : top + (i + 1) * tile, :count] for i in range(q)]
        right = [aug[top + i * tile : top + (i + 1) * tile, count:] for i in range(q)]
        for i in range(q):
            first = top + i * tile
            cols = {
                j: [jnp.broadcast_to(left[j][:, first + s : first + s + 1], (tile, count)) for s in range(tile)]
                for j in range(i, q)
            }
            roots = jnp.zeros((tile, count), F32)
            for t in range(tile):
                pick = lambda x: jnp.broadcast_to(x[t : t + 1, :], (tile, count))
                pivot = pick(cols[i][t])
                roots = jnp.where(row == t, lax.rsqrt(pivot), roots)
                over = 1.0 / pivot
                heads = {s: pick(cols[i][s]) for s in range(t + 1, tile)}
                head_left, head_right = pick(left[i]), pick(right[i])
                for j in range(i, q):
                    factor = cols[j][t] * over
                    if j == i:
                        factor = jnp.where(row > t, factor, 0.0)
                    for s in range(t + 1, tile):
                        cols[j][s] = cols[j][s] - factor * heads[s]
                    left[j] = left[j] - factor * head_left
                    right[j] = right[j] - factor * head_right
            left[i] = left[i] * roots
            right[i] = right[i] * roots
            out[first : first + tile, :] = right[i]
        low = top + block
        if low < count:
            upper = jnp.concatenate(left, axis=0)
            lane = lax.broadcasted_iota(jnp.int32, upper.shape, 1)
            both = jnp.concatenate([upper, jnp.concatenate(right, axis=0)], axis=1)
            change = dot(jnp.where(lane >= low, upper, 0.0), both, 0, 0)
            aug[low:, :] = aug[low:, :] - change[low:, :]


def basis_kernel(place, mine, other, deflated, *rest, scale):
    outs, aug, inverse = rest[:-2], rest[-2], rest[-1]
    count = deflated.shape[0]
    half = mine.shape[0]

    @pl.when(place[1] == 0)
    def _():
        aug[:half, :count] = mine[...]
        aug[half:, :count] = other[...]

    @pl.when(place[1] == 1)
    def _():
        aug[half:, :count] = mine[...]
        aug[:half, :count] = other[...]

    r = lax.broadcasted_iota(jnp.int32, (count, count), 0)
    c = lax.broadcasted_iota(jnp.int32, (count, count), 1)
    aug[:, count:] = jnp.where(r == c, 1.0, 0.0).astype(F32)
    lower_inverse(aug, inverse, count)
    rows, size, nx = outs[0].shape
    order = [
        inverse[pl.ds(pl.multiple_of((place[0] ^ k) * size, TILE), size), :] for k in range(len(outs))
    ]
    value = dot3(scale * jnp.concatenate(order, axis=0), deflated[...], 1, 0)
    for k, out in enumerate(outs):
        for i in range(rows):
            out[i] = value[k * size : (k + 1) * size, i * nx : (i + 1) * nx]


def place_kernel(place, *refs, near_share, far_share, near_rows):
    parts, out = refs[:-1], refs[-1]
    count, _ = parts[0].shape[1:]
    total = out.shape[0] // count
    for k, part in enumerate(parts):
        for i in range(near_share + far_share):
            if i < near_share:
                row = (place[0] ^ k) * near_share + i
            else:
                row = near_rows + (place[0] ^ k) * far_share + i - near_share
            out[pl.ds(row, count, stride=total), :] = part[i]


def groups_of(size, first):
    bits = []
    while first < size:
        bits.append(first)
        first *= 2
    out = []
    while bits:
        take, bits = bits[:2], bits[2:]
        out.append(take if len(take) == 1 else [take[0], take[1], take[0] | take[1]])
    return out


def summed(x, axis, first):
    for group in groups_of(lax.axis_size(axis), first):
        got = [swap(x, axis, bits) for bits in group]
        for g in got:
            x = x + g
    return x


def order_of(parts):
    far = [k for k in range(parts) if 2 * k >= parts]
    return far + [k for k in range(1, parts) if 2 * k < parts]


def per_device(start_block, locked_modes, material, support):
    depth, ny, nx = material.shape
    own_count, own_modes = start_block.shape[0], locked_modes.shape[0]
    parts = lax.axis_size("blk")
    slab, z = lax.axis_index("slab"), lax.axis_index("blk")
    place = jnp.stack([z, slab % 2]).astype(jnp.int32)
    rows = depth * ny
    far_share = max(1, rows // (4 * parts))
    far_rows = far_share * parts
    near_rows = rows - far_rows
    near_share = near_rows // parts
    count = own_count * parts
    ks = range(parts)
    order = order_of(parts)

    def exchanged(pieces):
        got = {k: swap(pieces[k], "blk", k) for k in order}
        return [got[k] if k else pieces[0] for k in ks]

    def gathered(piece):
        have, bit = {0: piece}, parts // 2
        while bit:
            got = {k ^ bit: swap(x, "blk", bit) for k, x in have.items()}
            have |= got
            bit //= 2
        return [have[k] for k in ks]

    modes = locked_modes.reshape(-1, nx)
    block = own_modes // 2 if own_modes % (2 * TILE) == 0 else own_modes
    near_modes = [None] * parts
    for some in (order[:1], order[1:]):
        got = split_modes(
            lambda *refs, total: near_kernel(*refs, total=total, ks=some),
            place,
            modes,
            [(near_share, own_modes, nx)] * len(some),
            block,
        )
        for k, x in zip(some, got):
            near_modes[k] = x
    start_block, near_modes[order[-1]] = lax.optimization_barrier([start_block, near_modes[order[-1]]])
    near_modes = exchanged(near_modes)
    near_modes[0], far_own, *far_modes = split_modes(
        far_kernel,
        place,
        modes,
        [(near_share, own_modes, nx), (far_rows, own_modes, nx)] + [(far_share, own_modes, nx)] * parts,
        block,
    )

    root_stiff = jnp.where(material == 1, 1.0, VOID_ROOT).astype(F32)
    clamped = jnp.where(slab == 0, support, 0).astype(F32)
    layer = lax.broadcasted_iota(jnp.int32, material.shape, 0)
    coef_own = jnp.where(layer == 0, 1.0 - clamped[None], 1.0) * root_stiff
    near_fields, far_field = filtered_rows(
        place, start_block, coef_own, clamped, near_rows, far_rows, parts
    )
    near_fields = exchanged(near_fields)
    far_fields = gathered(far_field)

    near_all, *sums = call(
        lambda *refs: near_correlate_kernel(*refs, parts=parts),
        place,
        near_modes + near_fields,
        [(near_share, count, nx)] + [(own_modes, count)] * parts,
    )
    sums = exchanged(sums)
    held = lax.optimization_barrier(far_modes + far_fields)
    far_modes, far_fields = held[:parts], held[parts:]
    far_modes = exchanged(far_modes)
    far_all, corr = call(
        lambda *refs: far_correlate_kernel(*refs, parts=parts),
        place,
        [far_own] + far_fields + sums,
        [(far_rows, count, nx), (own_modes, count)],
    )
    corr = corr + swap(corr, "slab", 1)
    corr = summed(corr, "slab", 2)
    corr = exchanged([corr] * parts)
    deflated, mine, other = call(
        lambda *refs: deflate_kernel(*refs, parts=parts),
        place,
        corr + near_modes + far_modes + [near_all, far_all],
        [(count, (near_share + far_share) * nx), (count // 2, count), (count // 2, count)],
    )
    gram = summed(summed(mine + swap(other, "slab", 1), "slab", 2), "blk", 1)
    total_cells = rows * nx * lax.axis_size("slab")
    scale = float(total_cells) ** 0.5
    outs = call(
        lambda *refs: basis_kernel(*refs, scale=scale),
        place,
        [gram, swap(gram, "slab", 1), deflated],
        [(near_share + far_share, own_count, nx)] * parts,
        scratch=[(count, 2 * count), (count, count)],
    )
    outs = exchanged(list(outs))
    basis = pl.pallas_call(
        lambda *refs: place_kernel(*refs, near_share=near_share, far_share=far_share, near_rows=near_rows),
        grid=(own_count // TILE,),
        in_specs=[smem()] + [pl.BlockSpec((near_share + far_share, TILE, nx), lambda g: (0, g, 0))] * parts,
        out_specs=pl.BlockSpec((TILE * rows, nx), lambda g: (g, 0)),
        out_shape=jax.ShapeDtypeStruct((own_count * rows, nx), F32),
        name="place",
    )(place, *outs)
    return basis.reshape(start_block.shape)


def solution(mesh):
    in_specs = (
        P("blk", "slab", None, None),
        P("blk", "slab", None, None),
        P("slab", None, None),
        P(),
    )
    out_specs = P("blk", "slab", None, None)

    return jax.shard_map(per_device, mesh=mesh, in_specs=in_specs, out_specs=out_specs, check_vma=False)
```

```python
import jax
import jax.numpy as jnp
from jax import lax
from jax.experimental import pallas as pl
from jax.experimental.pallas import tpu as pltpu
from jax.sharding import PartitionSpec as P

DEGREE = 8
THETA_LOAD = 0.1
VOID_ROOT = 0.31622776601683794
FILTER_CENTRE = 9.0
FILTER_HALF = 7.5


HIGHEST = lax.Precision.HIGHEST
F32 = jnp.float32
TILE = 8


def swap(x, axis, bits):
    return lax.ppermute(x, axis, [(i, i ^ bits) for i in range(lax.axis_size(axis))])


def whole(shape):
    return pl.BlockSpec(shape, lambda *_: (0,) * len(shape))


def smem():
    return pl.BlockSpec(memory_space=pltpu.SMEM)


def call(kernel, place, args, outs, scratch=()):
    return pl.pallas_call(
        kernel,
        in_specs=[smem()] + [whole(a.shape) for a in args],
        out_specs=[whole(s) for s in outs],
        out_shape=[jax.ShapeDtypeStruct(s, F32) for s in outs],
        scratch_shapes=[pltpu.VMEM(s, F32) for s in scratch],
    )(place, *args)


def dot(a, b, da, db):
    return lax.dot_general(
        a, b, (((da,), (db,)), ((), ())), precision=HIGHEST, preferred_element_type=F32
    )


def halved(x):
    high = x.astype(jnp.bfloat16)
    return high, (x - high.astype(F32)).astype(jnp.bfloat16)


def dot3(a, b, da, db):
    (ah, al), (bh, bl) = halved(a), halved(b)
    one = lambda x, y: lax.dot_general(
        x, y, (((da,), (db,)), ((), ())), preferred_element_type=F32
    )
    return one(ah, bh) + (one(ah, bl) + one(al, bh))


def in_line(ref):
    return jnp.concatenate([ref[r] for r in range(ref.shape[0])], axis=1)


def near_kernel(place, modes, *outs, total, ks):
    count = modes.shape[0] // total
    share = outs[0].shape[0]
    for k, out in zip(ks, outs):
        start = (place[0] ^ k) * share
        for i in range(share):
            out[i] = modes[pl.ds(start + i, count, stride=total), :]


def far_kernel(place, modes, near, far, *outs, total):
    count = modes.shape[0] // total
    share = near.shape[0]
    start = place[0] * share
    for i in range(share):
        near[i] = modes[pl.ds(start + i, count, stride=total), :]
    first = total - far.shape[0]
    for i in range(far.shape[0]):
        far[i] = modes[pl.ds(first + i, count, stride=total), :]
    share = outs[0].shape[0]
    for k, out in enumerate(outs):
        start = first + (place[0] ^ k) * share
        for i in range(share):
            out[i] = modes[pl.ds(start + i, count, stride=total), :]


def split_modes(kernel, place, modes, outs, block):
    total = modes.shape[0] // outs[0][1]
    nx = modes.shape[1]
    return pl.pallas_call(
        lambda *refs: kernel(*refs, total=total),
        grid=(outs[0][1] // block,),
        in_specs=[smem(), pl.BlockSpec((block * total, nx), lambda g: (g, 0))],
        out_specs=[pl.BlockSpec((s[0], block, nx), lambda g: (0, g, 0)) for s in outs],
        out_shape=[jax.ShapeDtypeStruct(s, F32) for s in outs],
    )(place, modes)


def filter_kernel(place, own, below, above, coef_own, coef_below, coef_above, clamped, *rest, steps, ny):
    outs, (one, two, square, mixed, back) = rest[:-5], rest[-5:]
    nx = own.shape[1]
    depth = coef_own.shape[0]
    halo = coef_below.shape[0]
    total = depth + 2 * halo
    scale = 2.0 / FILTER_HALF
    col = lax.broadcasted_iota(jnp.int32, (TILE, nx), 1)
    left = jnp.where(col > 0, 0.5, 0.0).astype(F32)
    right = jnp.where(col < nx - 1, 0.5, 0.0).astype(F32)
    bulk = F32(scale * (0.5 - FILTER_CENTRE))
    near = F32(THETA_LOAD)
    centre = F32(16.0 - 4.0 * THETA_LOAD)

    @pl.when(pl.program_id(0) == 0)
    def _():
        for i in range(total):
            if i < halo:
                coef = coef_below[i]
            elif i < halo + depth:
                coef = coef_own[i - halo]
            else:
                coef = coef_above[i - halo - depth]
            for y in range(ny):
                row = jnp.broadcast_to(coef[y : y + 1, :], (TILE, nx))
                weight = F32(scale) * row * row
                square[i, y] = weight
                mixed[i, y] = centre * weight + bulk
                if halo <= i < halo + depth:
                    back[i - halo, y] = jnp.where(row > 0, 1.0 / jnp.where(row > 0, row, 1.0), 0.0)

    for i in range(total):
        if i < halo:
            source, base, layers, coef = below, i, halo, coef_below[i]
        elif i < halo + depth:
            source, base, layers, coef = own, i - halo, depth, coef_own[i - halo]
        else:
            source, base, layers, coef = above, i - halo - depth, halo, coef_above[i - halo - depth]
        for y in range(ny):
            value = source[pl.ds(base * ny + y, TILE, stride=layers * ny), :]
            one[i, y] = jnp.broadcast_to(coef[y : y + 1, :], (TILE, nx)) * value

    current, previous = one, two
    for step in range(steps):
        lo, hi = step + 1, total - 1 - step

        def layer(i, carry, step=step, current=current, previous=previous):
            here, pair = carry
            after = [current[i + 1, y] for y in range(ny)]
            pair_after = [here[y] + after[y] for y in range(ny)]
            line = [pair[y] + pair_after[y] for y in range(ny)]
            across = [line[y] + line[y + 1] for y in range(ny - 1)]
            for y in range(ny):
                if y == 0:
                    plane = across[0] + line[0]
                elif y == ny - 1:
                    plane = across[y - 1] + line[y]
                else:
                    plane = across[y - 1] + across[y]
                cube = plane + left * pltpu.roll(plane, 1, 1) + right * pltpu.roll(plane, nx - 1, 1)
                new = mixed[i, y] * here[y] + square[i, y] * (near * line[y] - 0.5 * cube)
                if step == 0:
                    previous[i, y] = 0.5 * new
                else:
                    previous[i, y] = new - previous[i, y]
            return after, pair_after

        before = [current[lo - 1, y] for y in range(ny)]
        here = [current[lo, y] for y in range(ny)]
        carry = (here, [before[y] + here[y] for y in range(ny)])
        for i in range(lo, hi):
            carry = layer(i, carry)
        current, previous = previous, current

    before, now = 1.0, (1.0 - FILTER_CENTRE) / FILTER_HALF
    for _ in range(steps - 1):
        before, now = now, 2.0 * now * (1.0 - FILTER_CENTRE) / FILTER_HALF - before
    for i in range(depth):
        for y in range(ny):
            value = back[i, y] * current[halo + i, y]
            if i == 0:
                fixed = jnp.broadcast_to(clamped[y : y + 1, :], (TILE, nx))
                value = value + F32(now) * fixed * own[pl.ds(y, TILE, stride=depth * ny), :]
            previous[i, y] = value
    rows = previous.reshape(total * ny, TILE, nx)
    far = outs[-1]
    far[...] = rows[pl.ds(depth * ny - far.shape[0], far.shape[0])]
    for k, out in enumerate(outs[:-1]):
        out[...] = rows[pl.ds((place[0] ^ k) * out.shape[0], out.shape[0])]


def filtered_rows(place, start_block, coef_own, clamped, near_rows, far_rows, parts):
    count, depth, ny, nx = start_block.shape
    halo = DEGREE
    assert depth >= halo and count % TILE == 0
    slabs = lax.axis_size("slab")
    rise = [(i, i + 1) for i in range(slabs - 1)]
    fall = [(i + 1, i) for i in range(slabs - 1)]
    below = lax.ppermute(start_block[:, depth - halo :], "slab", rise)
    above = lax.ppermute(start_block[:, :halo], "slab", fall)
    coef_below = lax.ppermute(coef_own[depth - halo :], "slab", rise)
    coef_above = lax.ppermute(coef_own[:halo], "slab", fall)
    outs = [(near_rows // parts, count, nx)] * parts + [(far_rows, count, nx)]
    total = depth + 2 * halo
    got = pl.pallas_call(
        lambda *refs: filter_kernel(*refs, steps=DEGREE, ny=ny),
        grid=(count // TILE,),
        in_specs=[smem()]
        + [pl.BlockSpec((TILE * n * ny, nx), lambda g: (g, 0)) for n in (depth, halo, halo)]
        + [whole(c.shape) for c in (coef_own, coef_below, coef_above, clamped)],
        out_specs=[pl.BlockSpec((s[0], TILE, nx), lambda g: (0, g, 0)) for s in outs],
        out_shape=[jax.ShapeDtypeStruct(s, F32) for s in outs],
        scratch_shapes=[pltpu.VMEM((total, ny, TILE, nx), F32)] * 4 + [pltpu.VMEM((depth, ny, TILE, nx), F32)],
        name="chebyshev",
    )(
        place,
        start_block.reshape(-1, nx),
        below.reshape(-1, nx),
        above.reshape(-1, nx),
        coef_own,
        coef_below,
        coef_above,
        clamped,
    )
    return list(got[:-1]), got[-1]


def gather_fields(place, parts, fields):
    count = parts[0].shape[1]
    for k, part in enumerate(parts):
        start = pl.multiple_of((place[0] ^ k) * count, TILE)
        fields[:, pl.ds(start, count), :] = part[...]


def near_correlate_kernel(place, *refs, parts):
    modes, pieces, fields, outs = refs[:parts], refs[parts : 2 * parts], refs[2 * parts], refs[2 * parts + 1 :]
    gather_fields(place, pieces, fields)
    own = in_line(fields)
    stack = jnp.concatenate([in_line(m) for m in modes], axis=0)
    value = dot3(stack, own, 1, 1)
    size = outs[0].shape[0]
    for k, out in enumerate(outs):
        out[...] = value[k * size : (k + 1) * size]


def far_correlate_kernel(place, modes, *refs, parts):
    pieces, sums, fields, out = refs[:parts], refs[parts : 2 * parts], refs[2 * parts], refs[2 * parts + 1]
    gather_fields(place, pieces, fields)
    value = dot3(in_line(modes), in_line(fields), 1, 1)
    for s in sums:
        value = value + s[...]
    out[...] = value


def halves(core, value, mine, other):
    size = mine.shape[0]

    @pl.when(core == 0)
    def _():
        mine[...] = value[:size]
        other[...] = value[size:]

    @pl.when(core == 1)
    def _():
        mine[...] = value[size:]
        other[...] = value[:size]


def deflate_kernel(place, *refs, parts):
    corr, near, far = refs[:parts], refs[parts : 2 * parts], refs[2 * parts : 3 * parts]
    near_fields, far_fields, deflated, mine, other = refs[3 * parts :]
    share = far[0].shape[0]
    fields = [near_fields[r] for r in range(near_fields.shape[0])]
    fields += [far_fields[place[0] * share + r] for r in range(share)]
    modes = jnp.concatenate(
        [jnp.concatenate([in_line(a), in_line(b)], axis=1) for a, b in zip(near, far)], axis=0
    )
    stack = jnp.concatenate([c[...] for c in corr], axis=0)
    value = jnp.concatenate(fields, axis=1) - dot3(stack, modes, 0, 0)
    deflated[...] = value
    halves(place[1], dot3(value, value, 1, 1), mine, other)


def lower_inverse(aug, out, count):
    tile, block = TILE, min(64, count)
    row = lax.broadcasted_iota(jnp.int32, (tile, count), 0)
    for top in range(0, count, block):
        q = block // tile
        left = [aug[top + i * tile : top + (i + 1) * tile, :count] for i in range(q)]
        right = [aug[top + i * tile : top + (i + 1) * tile, count:] for i in range(q)]
        for i in range(q):
            first = top + i * tile
            cols = {
                j: [jnp.broadcast_to(left[j][:, first + s : first + s + 1], (tile, count)) for s in range(tile)]
                for j in range(i, q)
            }
            roots = jnp.zeros((tile, count), F32)
            for t in range(tile):
                pick = lambda x: jnp.broadcast_to(x[t : t + 1, :], (tile, count))
                pivot = pick(cols[i][t])
                roots = jnp.where(row == t, lax.rsqrt(pivot), roots)
                over = 1.0 / pivot
                heads = {s: pick(cols[i][s]) for s in range(t + 1, tile)}
                head_left, head_right = pick(left[i]), pick(right[i])
                for j in range(i, q):
                    factor = cols[j][t] * over
                    if j == i:
                        factor = jnp.where(row > t, factor, 0.0)
                    for s in range(t + 1, tile):
                        cols[j][s] = cols[j][s] - factor * heads[s]
                    left[j] = left[j] - factor * head_left
                    right[j] = right[j] - factor * head_right
            left[i] = left[i] * roots
            right[i] = right[i] * roots
            out[first : first + tile, :] = right[i]
        low = top + block
        if low < count:
            upper = jnp.concatenate(left, axis=0)
            lane = lax.broadcasted_iota(jnp.int32, upper.shape, 1)
            both = jnp.concatenate([upper, jnp.concatenate(right, axis=0)], axis=1)
            change = dot(jnp.where(lane >= low, upper, 0.0), both, 0, 0)
            aug[low:, :] = aug[low:, :] - change[low:, :]


def basis_kernel(place, mine, other, deflated, *rest, scale):
    outs, aug, inverse = rest[:-2], rest[-2], rest[-1]
    count = deflated.shape[0]
    half = mine.shape[0]

    @pl.when(place[1] == 0)
    def _():
        aug[:half, :count] = mine[...]
        aug[half:, :count] = other[...]

    @pl.when(place[1] == 1)
    def _():
        aug[half:, :count] = mine[...]
        aug[:half, :count] = other[...]

    r = lax.broadcasted_iota(jnp.int32, (count, count), 0)
    c = lax.broadcasted_iota(jnp.int32, (count, count), 1)
    aug[:, count:] = jnp.where(r == c, 1.0, 0.0).astype(F32)
    lower_inverse(aug, inverse, count)
    rows, size, nx = outs[0].shape
    order = [
        inverse[pl.ds(pl.multiple_of((place[0] ^ k) * size, TILE), size), :] for k in range(len(outs))
    ]
    value = dot3(scale * jnp.concatenate(order, axis=0), deflated[...], 1, 0)
    for k, out in enumerate(outs):
        for i in range(rows):
            out[i] = value[k * size : (k + 1) * size, i * nx : (i + 1) * nx]


def place_kernel(place, *refs, near_share, far_share, near_rows):
    parts, out = refs[:-1], refs[-1]
    count, _ = parts[0].shape[1:]
    total = out.shape[0] // count
    for k, part in enumerate(parts):
        for i in range(near_share + far_share):
            if i < near_share:
                row = (place[0] ^ k) * near_share + i
            else:
                row = near_rows + (place[0] ^ k) * far_share + i - near_share
            out[pl.ds(row, count, stride=total), :] = part[i]


def groups_of(size, first):
    bits = []
    while first < size:
        bits.append(first)
        first *= 2
    out = []
    while bits:
        take, bits = bits[:2], bits[2:]
        out.append(take if len(take) == 1 else [take[0], take[1], take[0] | take[1]])
    return out


def summed(x, axis, first):
    for group in groups_of(lax.axis_size(axis), first):
        got = [swap(x, axis, bits) for bits in group]
        for g in got:
            x = x + g
    return x


def order_of(parts):
    far = [k for k in range(parts) if 2 * k >= parts]
    return far + [k for k in range(1, parts) if 2 * k < parts]


def per_device(start_block, locked_modes, material, support):
    depth, ny, nx = material.shape
    own_count, own_modes = start_block.shape[0], locked_modes.shape[0]
    parts = lax.axis_size("blk")
    slab, z = lax.axis_index("slab"), lax.axis_index("blk")
    place = jnp.stack([z, slab % 2]).astype(jnp.int32)
    rows = depth * ny
    far_share = max(1, rows // (4 * parts))
    far_rows = far_share * parts
    near_rows = rows - far_rows
    near_share = near_rows // parts
    count = own_count * parts
    ks = range(parts)
    order = order_of(parts)

    def exchanged(pieces):
        got = {k: swap(pieces[k], "blk", k) for k in order}
        return [got[k] if k else pieces[0] for k in ks]

    def gathered(piece):
        have, bit = {0: piece}, parts // 2
        while bit:
            got = {k ^ bit: swap(x, "blk", bit) for k, x in have.items()}
            have |= got
            bit //= 2
        return [have[k] for k in ks]

    modes = locked_modes.reshape(-1, nx)
    block = own_modes // 2 if own_modes % (2 * TILE) == 0 else own_modes
    near_modes = [None] * parts
    for some in (order[:1], order[1:]):
        got = split_modes(
            lambda *refs, total: near_kernel(*refs, total=total, ks=some),
            place,
            modes,
            [(near_share, own_modes, nx)] * len(some),
            block,
        )
        for k, x in zip(some, got):
            near_modes[k] = x
    start_block, near_modes[order[-1]] = lax.optimization_barrier([start_block, near_modes[order[-1]]])
    near_modes = exchanged(near_modes)
    near_modes[0], far_own, *far_modes = split_modes(
        far_kernel,
        place,
        modes,
        [(near_share, own_modes, nx), (far_rows, own_modes, nx)] + [(far_share, own_modes, nx)] * parts,
        block,
    )

    root_stiff = jnp.where(material == 1, 1.0, VOID_ROOT).astype(F32)
    clamped = jnp.where(slab == 0, support, 0).astype(F32)
    layer = lax.broadcasted_iota(jnp.int32, material.shape, 0)
    coef_own = jnp.where(layer == 0, 1.0 - clamped[None], 1.0) * root_stiff
    near_fields, far_field = filtered_rows(
        place, start_block, coef_own, clamped, near_rows, far_rows, parts
    )
    near_fields = exchanged(near_fields)
    far_fields = gathered(far_field)

    near_all, *sums = call(
        lambda *refs: near_correlate_kernel(*refs, parts=parts),
        place,
        near_modes + near_fields,
        [(near_share, count, nx)] + [(own_modes, count)] * parts,
    )
    sums = exchanged(sums)
    held = lax.optimization_barrier(far_modes + far_fields)
    far_modes, far_fields = held[:parts], held[parts:]
    far_modes = exchanged(far_modes)
    far_all, corr = call(
        lambda *refs: far_correlate_kernel(*refs, parts=parts),
        place,
        [far_own] + far_fields + sums,
        [(far_rows, count, nx), (own_modes, count)],
    )
    corr = corr + swap(corr, "slab", 1)
    corr = summed(corr, "slab", 2)
    corr = exchanged([corr] * parts)
    deflated, mine, other = call(
        lambda *refs: deflate_kernel(*refs, parts=parts),
        place,
        corr + near_modes + far_modes + [near_all, far_all],
        [(count, (near_share + far_share) * nx), (count // 2, count), (count // 2, count)],
    )
    gram = summed(summed(mine + swap(other, "slab", 1), "slab", 2), "blk", 1)
    total_cells = rows * nx * lax.axis_size("slab")
    scale = float(total_cells) ** 0.5
    outs = call(
        lambda *refs: basis_kernel(*refs, scale=scale),
        place,
        [gram, swap(gram, "slab", 1), deflated],
        [(near_share + far_share, own_count, nx)] * parts,
        scratch=[(count, 2 * count), (count, count)],
    )
    outs = exchanged(list(outs))
    (basis,) = call(
        lambda *refs: place_kernel(*refs, near_share=near_share, far_share=far_share, near_rows=near_rows),
        place,
        outs,
        [(own_count * rows, nx)],
    )
    return basis.reshape(start_block.shape)


def solution(mesh):
    in_specs = (
        P("blk", "slab", None, None),
        P("blk", "slab", None, None),
        P("slab", None, None),
        P(),
    )
    out_specs = P("blk", "slab", None, None)

    return jax.shard_map(
        per_device, mesh=mesh, in_specs=in_specs, out_specs=out_specs, check_vma=False
    )
```
